32 devices in a mesh: clip: 2 (over x), ha: 4 (over z), wa: 4 (over y, core).
Axes of the slice: x: 2, y: 2, z: 4, core: 2. Of those that a mesh axis runs over, the one named last changes fastest.
Arguments:
- latent_cond: bfloat16 [2, 1, 64, 64, 2560], P('clip', None, 'ha', 'wa')
- latent_uncond: bfloat16 [2, 1, 64, 64, 2560], P('clip', None, 'ha', 'wa')
- qkv_weight: bfloat16 [2560, 3840], P(('clip', 'ha', 'wa')), may hold values from -0.125 to 0.125
- cond_pairs: bfloat16 [2, 2, 256, 1280], P('clip', None, ('ha', 'wa')), may hold values from -6 to 6
- guide_mask: int32 [2, 16], P('clip', ('ha', 'wa')), may hold values 0 or 1
- shifts: int32 [2, 2], P('clip'), may hold values from -4 to 4, as said below
- kernel: float32 [3, 3, 1280], replicated, may hold values from -1.2 to 1.2
Outputs:
- refined: bfloat16 [2, 2, 1, 64, 64, 1280], P('clip', None, None, 'ha', 'wa')
The draws below stay inside these ranges and needn't reach their ends.
Inputs may be any that keep to these rules, and one draw needn't show every extreme that they name: `shifts`: in every draw clip 0 has row shift 4 and column shift -4.
All inputs are finite; a program needn't handle non-finite values. No bound on the sum of `guide_mask` on one device may be relied on, other than what follows from the above.
Results may differ from the reference program's by a relative error of at most 0.011.
Values may be sent and summed in bfloat16 or wider, within the bound.
No kernel may reach another device: no remote copies, remote signals or barrier semaphores. Data moves between devices by JAX's collectives and lax.ppermute only.
A program may use at most 128 MiB of HBM per device.

```python
import math
import jax
import jax.numpy as jnp
from jax import lax

D = 2560
HEADS = 10
HD = 128
WIN = 8
FRAMES = 1
CLIPS = 2
HEIGHT = 64
WIDTH = 64
NC = 256
REGIONS = 16
N_HA = 4
N_WA = 4


def draw_latent(key):
    shape = (CLIPS, FRAMES, HEIGHT, WIDTH, D)
    noise = jax.random.truncated_normal(jax.random.fold_in(key, 0), -6.0, 6.0, shape, jnp.float32)
    return noise.astype(jnp.bfloat16)


def draw_latent_cond(key, part):
    return draw_latent(jax.random.fold_in(key, 101))


def draw_latent_uncond(key, part):
    return draw_latent(jax.random.fold_in(key, 202))


def draw_shifts(key, part):
    limit = WIN // 2
    values = jax.random.randint(jax.random.fold_in(key, 303), (CLIPS, 2), -limit, limit + 1, jnp.int32)
    values = values.at[0, 0].set(limit)
    return values.at[0, 1].set(-limit)


def plant(drawn, own_key, low, largest):
    index_at = [jax.random.randint(jax.random.fold_in(own_key, axis), (), 0, length) for axis, length in enumerate(drawn.shape)]
    widest = drawn.shape.index(max(drawn.shape))
    neighbour = index_at[:widest] + [(index_at[widest] + 1) % drawn.shape[widest]] + index_at[widest + 1:]
    return drawn.at[tuple(index_at)].set(low).at[tuple(neighbour)].set(largest)


def block_scale(own_key, dims, pieces, smallest, top_value):
    def one(axis_at, parts):
        draws = jax.random.uniform(jax.random.fold_in(jax.random.fold_in(own_key, 6), axis_at), (parts,), jnp.float32, smallest / len(pieces), top_value / len(pieces))
        return jnp.repeat(jnp.exp(draws), dims[axis_at] // parts).reshape((-1,) + (1,) * (len(dims) - axis_at - 1))

    loudness = one(*pieces[0])
    for cut in pieces[1:]:
        loudness = loudness * one(*cut)
    return loudness


def centred(own_key, shape, scale, bound, pieces=(), kind=jnp.bfloat16):
    values = scale * jax.random.normal(own_key, shape, jnp.float32)
    if pieces:
        values = values * block_scale(own_key, shape, pieces, -0.22, 0.18)
    return jnp.clip(values, -bound, bound).astype(kind)


def setup_inputs(seed: int = 0) -> dict:
    arg_keys = jax.random.split(jax.random.key(seed), 8)
    latent_cond = draw_latent_cond(jax.random.fold_in(arg_keys[7], 71), 0)
    latent_uncond = draw_latent_uncond(jax.random.fold_in(arg_keys[7], 71), 0)
    qkv_weight = centred(arg_keys[2], (D, 3 * HEADS * HD), D ** -0.5, 0.125, ((0, 32),))
    cond_pairs = centred(arg_keys[3], (CLIPS, 2, NC, HEADS * HD), 1.0, 6.0, ((0, 2), (2, 16)))
    guide_mask = plant((jax.random.randint(arg_keys[4], (CLIPS, REGIONS), 0, 2) < 1).astype(jnp.int32), jax.random.fold_in(arg_keys[4], 1), 0, 1)
    shifts = draw_shifts(jax.random.fold_in(arg_keys[7], 71), 0)
    kernel = centred(arg_keys[6], (3, 3, HEADS * HD), 0.3, 1.2, (), jnp.float32)
    return dict(latent_cond=latent_cond, latent_uncond=latent_uncond, qkv_weight=qkv_weight, cond_pairs=cond_pairs, guide_mask=guide_mask, shifts=shifts, kernel=kernel)


def to_windows(grid_field):
    frames, height, width, channels = grid_field.shape
    grid_field = grid_field.reshape(frames, height // WIN, WIN, width // WIN, WIN, channels)
    grid_field = grid_field.transpose(0, 1, 3, 2, 4, 5)
    return grid_field.reshape(-1, WIN * WIN, channels)

def from_windows(blocks, frames, height, width):
    channels = blocks.shape[-1]
    grid_field = blocks.reshape(frames, height // WIN, width // WIN, WIN, WIN, channels)
    return grid_field.transpose(0, 1, 3, 2, 4, 5).reshape(frames, height, width, channels)

def attend(blocks, cond_pair):
    win_count, win_tokens, _ = blocks.shape
    channels = HEADS * HD
    score_scale = 1.0 / math.sqrt(HD)
    blocks = blocks.astype(jnp.float32)
    queries = blocks[:, :, :channels].reshape(win_count, win_tokens, HEADS, HD)
    key_rows = blocks[:, :, channels:2 * channels].reshape(win_count, win_tokens, HEADS, HD)
    values = blocks[:, :, 2 * channels:].reshape(win_count, win_tokens, HEADS, HD)
    scores = jnp.einsum('wqhd,wkhd->whqk', queries, key_rows) * score_scale
    if cond_pair is None:
        top_score = lax.optimization_barrier(jnp.max(scores, axis=-1, keepdims=True))
        near_exp = jnp.exp(scores - top_score)
        near_weights = lax.optimization_barrier((near_exp / lax.optimization_barrier(jnp.sum(near_exp, axis=-1, keepdims=True))).astype(jnp.bfloat16))
        attended = jnp.einsum('whqk,wkhd->wqhd', near_weights.astype(jnp.float32), values)
    else:
        cond_keys = cond_pair[0].astype(jnp.float32).reshape(-1, HEADS, HD)
        cond_values = cond_pair[1].astype(jnp.float32).reshape(-1, HEADS, HD)
        far_scores = jnp.einsum('wqhd,khd->whqk', queries, cond_keys) * score_scale
        top_score = jnp.maximum(lax.optimization_barrier(jnp.max(scores, axis=-1, keepdims=True)), lax.optimization_barrier(jnp.max(far_scores, axis=-1, keepdims=True)))
        near_exp = jnp.exp(scores - top_score)
        far_exp = jnp.exp(far_scores - top_score)
        denom = lax.optimization_barrier(jnp.sum(near_exp, axis=-1, keepdims=True)) + lax.optimization_barrier(jnp.sum(far_exp, axis=-1, keepdims=True))
        near_weights = lax.optimization_barrier((near_exp / denom).astype(jnp.bfloat16))
        far_weights = lax.optimization_barrier((far_exp / denom).astype(jnp.bfloat16))
        attended = jnp.einsum('whqk,wkhd->wqhd', near_weights.astype(jnp.float32), values)
        attended = attended + jnp.einsum('whqk,khd->wqhd', far_weights.astype(jnp.float32), cond_values)
    return attended.reshape(win_count, win_tokens, channels).astype(jnp.bfloat16)

def refine(grid_field, kernel):
    frames, height, width, channels = grid_field.shape
    widened = grid_field.astype(jnp.float32)
    padded = jnp.pad(widened, ((0, 0), (1, 1), (1, 1), (0, 0)))
    summed = widened
    for row_tap in range(3):
        for col_tap in range(3):
            summed = summed + kernel[row_tap, col_tap] * padded[:, row_tap:row_tap + height, col_tap:col_tap + width, :]
    return summed.astype(jnp.bfloat16)

def reference(latent_cond, latent_uncond, qkv_weight, cond_pairs, guide_mask, shifts, kernel):
    tile_side = HEIGHT // N_HA

    def one_clip(clip_args):
        lat_cond, lat_uncond, cond_pair, region_flags, shift_pair = clip_args
        shift_rows = shift_pair[0]
        shift_cols = shift_pair[1]
        flag_grid = region_flags.reshape(N_HA, N_WA).astype(jnp.bfloat16)
        flag_grid = jnp.repeat(jnp.repeat(flag_grid, tile_side, axis=0), tile_side, axis=1)

        def project(latent):
            flat = latent.reshape(-1, D)
            product = jnp.dot(flat, qkv_weight, preferred_element_type=jnp.float32).astype(jnp.bfloat16)
            return product.reshape(FRAMES, HEIGHT, WIDTH, 3 * HEADS * HD)

        def branch(latent, pair, gating):
            shifted = jnp.roll(project(latent), -shift_rows, axis=1)
            shifted = jnp.roll(shifted, -shift_cols, axis=2)
            attended = from_windows(attend(to_windows(shifted), pair), FRAMES, HEIGHT, WIDTH)
            if gating is not None:
                attended = attended * gating[None, :, :, None]
            attended = jnp.roll(attended, shift_rows, axis=1)
            return jnp.roll(attended, shift_cols, axis=2)
        cond_attn = branch(lat_cond, cond_pair, None)
        uncond_attn = branch(lat_uncond, None, flag_grid)
        return jnp.stack([refine(cond_attn, kernel), refine(uncond_attn, kernel)])
    return lax.map(one_clip, (latent_cond, latent_uncond, cond_pairs, guide_mask, shifts))
```

```python
import functools
import math

import jax
import jax.numpy as jnp
from jax import lax
from jax.experimental import pallas as pl
from jax.experimental.pallas import tpu as pltpu
from jax.sharding import Mesh
from jax.sharding import PartitionSpec as P

HEADS = 10
HD = 128
WIN = 8
RIM = WIN // 2
CHUNKS = (3, 2)


def cyc(x, axis, step):
    count = lax.axis_size(axis)
    return lax.ppermute(x, axis, [(i, (i + step) % count) for i in range(count)])


def ordered(flag, mine, other, axis):
    first = jnp.where(flag == 0, mine, other)
    second = jnp.where(flag == 0, other, mine)
    return jnp.concatenate([first, second], axis=axis)


def core_halves(block, heads, first, count):
    core = lax.axis_index("core")
    half = heads // 2
    shape = block.shape[:2] + (count, HD)
    mine = lax.dynamic_slice(block, (0, 0, core * half + first, 0), shape)
    other = lax.dynamic_slice(block, (0, 0, (1 - core) * half + first, 0), shape)
    flat = (block.shape[0], block.shape[1] * count * HD)
    return mine.reshape(flat), other.reshape(flat)


def gathered_weight(weight, heads, first, count):
    rows = weight.shape[0]
    mine, other = core_halves(weight.reshape(rows, 3, heads, HD), heads, first, count)
    got = cyc(other, "core", 1)
    block = ordered(lax.axis_index("core"), mine, got, 0)
    clips, has, wys = (lax.axis_size(a) for a in ("clip", "ha", "wy"))
    if clips != 2 or wys != 2:
        return lax.all_gather(block, ("clip", "ha", "wy"), axis=0, tiled=True)
    side = 2 * rows
    clip, ha, wy = (lax.axis_index(a) for a in ("clip", "ha", "wy"))
    near = [block] + [cyc(block, "ha", d) for d in range(1, has)]
    rest = jnp.concatenate(near[1:], axis=0)
    full = jnp.zeros((2 * has * 2 * side, block.shape[1]), block.dtype)

    def put(full, piece, c, d, y, skip=0):
        at = ((c * has + (ha - d) % has) * 2 + y) * side + skip
        return lax.dynamic_update_slice(full, piece, (at, 0))

    def put_all(full, own, others, c, y):
        full = put(full, own, c, 0, y)
        for d in range(1, has):
            full = put(full, others[(d - 1) * side : d * side], c, d, y)
        return full

    x_own, y_own = cyc(block, "clip", 1), cyc(block, "wy", 1)
    x_rest, y_rest = cyc(rest, "clip", 1), cyc(rest, "wy", 1)
    mid = rest.shape[0] // 2
    xy_own = jnp.concatenate(
        [cyc(x_own[:rows], "wy", 1), cyc(y_own[rows:], "clip", 1)], axis=0
    )
    xy_rest = jnp.concatenate(
        [cyc(x_rest[:mid], "wy", 1), cyc(y_rest[mid:], "clip", 1)], axis=0
    )
    full = put_all(full, block, rest, clip, wy)
    full = put_all(full, x_own, x_rest, 1 - clip, wy)
    full = put_all(full, y_own, y_rest, clip, 1 - wy)
    return put_all(full, xy_own, xy_rest, 1 - clip, 1 - wy)


def gathered_pairs(pairs, heads):
    kinds, rows, _ = pairs.shape
    block = pairs.transpose(1, 0, 2).reshape(rows, kinds, heads, HD)
    mine, other = core_halves(block, heads, 0, heads // 2)
    both = jnp.concatenate([mine, cyc(other, "core", 1)], axis=0)
    for axis in ("ha", "wy"):
        steps = range(1, lax.axis_size(axis))
        both = jnp.concatenate([both] + [cyc(both, axis, d) for d in steps], axis=0)
    return both


def attend_kernel(info, q_ref, k_ref, v_ref, fk_ref, fv_ref, out_ref, bias_ref, *, width):
    scale = 1.0 / math.sqrt(HD)
    tokens = q_ref.shape[0]
    shift = info[0]

    def window(shape, axis):
        slot = lax.broadcasted_iota(jnp.int32, shape, axis) & (width - 1)
        return ((slot - shift) & (width - 1)) >> 3

    @pl.when((pl.program_id(0) == 0) & (pl.program_id(1) == 0))
    def _():
        same = window((tokens, tokens), 0) == window((tokens, tokens), 1)
        bias_ref[...] = jnp.where(same, 0.0, -jnp.inf)

    def product(a, b):
        return lax.dot_general(
            a, b, (((1,), (1,)), ((), ())), preferred_element_type=jnp.float32
        )

    q = q_ref[...]
    near = product(q, k_ref[...]) * scale + bias_ref[...]

    @pl.when(pl.program_id(1) < 2)
    def _():
        far = product(q, fk_ref[...]) * scale
        top = jnp.maximum(
            jnp.max(near, axis=-1, keepdims=True), jnp.max(far, axis=-1, keepdims=True)
        )
        near_exp = jnp.exp(near - top)
        far_exp = jnp.exp(far - top)
        total = jnp.sum(near_exp, axis=-1, keepdims=True) + jnp.sum(
            far_exp, axis=-1, keepdims=True
        )
        mixed = jnp.dot(
            near_exp.astype(jnp.bfloat16), v_ref[...], preferred_element_type=jnp.float32
        ) + jnp.dot(
            far_exp.astype(jnp.bfloat16), fv_ref[...], preferred_element_type=jnp.float32
        )
        out_ref[...] = (mixed / total).astype(out_ref.dtype)

    @pl.when(pl.program_id(1) >= 2)
    def _():
        near_exp = jnp.exp(near - jnp.max(near, axis=-1, keepdims=True))
        total = jnp.sum(near_exp, axis=-1, keepdims=True)
        mixed = jnp.dot(
            near_exp.astype(jnp.bfloat16), v_ref[...], preferred_element_type=jnp.float32
        )
        keep = jnp.where(window((tokens, 1), 0) < width // 16, info[1], info[2]) > 0
        out_ref[...] = jnp.where(keep, mixed / total, 0.0).astype(out_ref.dtype)


def attend(info, projected, far, first, count, width):
    tokens = projected.shape[0] // 4
    all_heads = far.shape[1] // (2 * HD)

    def near_spec(offset):
        return pl.BlockSpec((tokens, HD), lambda i, j, s: (j, offset + i))

    def far_spec(offset):
        return pl.BlockSpec((far.shape[0], HD), lambda i, j, s: (0, offset + first + i))

    keys = 2 * tokens + 2 * far.shape[0]
    return pl.pallas_call(
        functools.partial(attend_kernel, width=width),
        grid_spec=pltpu.PrefetchScalarGridSpec(
            num_scalar_prefetch=1,
            grid=(count, 4),
            in_specs=[
                near_spec(0),
                near_spec(count),
                near_spec(2 * count),
                far_spec(0),
                far_spec(all_heads),
            ],
            out_specs=pl.BlockSpec((tokens, HD), lambda i, j, s: (j, i)),
            scratch_shapes=[pltpu.VMEM((tokens, tokens), jnp.float32)],
        ),
        out_shape=jax.ShapeDtypeStruct((4 * tokens, count * HD), jnp.bfloat16),
        cost_estimate=pl.CostEstimate(
            flops=8 * count * tokens * keys * HD,
            transcendentals=2 * count * tokens * keys,
            bytes_accessed=2 * projected.size * 2,
        ),
    )(info, projected, projected, projected, far, far)


def shifted_tokens(lat_cond, lat_uncond, shift_rows, shift_cols):
    core = lax.axis_index("core")
    rows, cols, _ = lat_cond.shape
    own = jnp.stack([lat_cond, lat_uncond])
    below = cyc(own[:, :RIM], "ha", -1)
    above = cyc(own[:, rows - RIM :], "ha", 1)
    tall = jnp.concatenate([above, own, below], axis=1)
    tile = lax.dynamic_slice_in_dim(tall, RIM + shift_rows, rows, axis=1)
    edge = jnp.where(core == 0, tile[:, :, :RIM], tile[:, :, cols - RIM :])
    across = cyc(edge, "wy", 1)
    blank = jnp.zeros(tile.shape[:2] + (cols - RIM,) + tile.shape[3:], tile.dtype)
    across = jnp.where(
        core == 0,
        jnp.concatenate([across, blank], axis=2),
        jnp.concatenate([blank, across], axis=2),
    )
    slot = lax.broadcasted_iota(jnp.int32, (1, 1, cols, 1), 2) + core * cols
    tile = jnp.where((slot < shift_cols) | (slot >= 2 * cols + shift_cols), across, tile)
    return ordered(core, tile, cyc(tile, "core", 1), 2)


def refined_part(attended, taps, shift_rows, shift_cols):
    _, rows, cols, _ = attended.shape
    rim = RIM + 1
    above = cyc(attended[:, rows - rim :], "ha", 1)
    below = cyc(attended[:, :rim], "ha", -1)
    tall = jnp.concatenate([above, attended, below], axis=1)
    tall = lax.dynamic_slice_in_dim(tall, RIM - shift_rows, rows + 2, axis=1)
    ha, wy = lax.axis_index("ha"), lax.axis_index("wy")
    row = lax.broadcasted_iota(jnp.int32, (1, rows + 2, 1, 1), 1)
    inside = ((row > 0) | (ha > 0)) & ((row < rows + 1) | (ha < lax.axis_size("ha") - 1))
    tall = jnp.where(inside, tall, jnp.zeros_like(tall))
    first, last = tall[:, :, :1], tall[:, :, cols - 1 :]
    sent = jnp.where(
        shift_cols >= 0,
        jnp.concatenate([tall[:, :, :RIM], last], axis=2),
        jnp.concatenate([tall[:, :, cols - RIM :], first], axis=2),
    )
    got = cyc(sent, "wy", 1)
    blank = jnp.zeros(tall.shape[:2] + (cols - 2 * RIM,) + tall.shape[3:], tall.dtype)
    spread = jnp.concatenate([got[:, :, :RIM], blank, got[:, :, :RIM]], axis=2)
    slot = lax.broadcasted_iota(jnp.int32, (1, 1, cols, 1), 2)
    centre = jnp.where((slot < shift_cols) | (slot >= cols + shift_cols), spread, tall)
    left = jnp.where(shift_cols < 0, last, got[:, :, RIM:])
    right = jnp.where(
        shift_cols > 0, first, jnp.where(shift_cols < 0, got[:, :, RIM:], got[:, :, :1])
    )
    left = jnp.where(wy > 0, left, jnp.zeros_like(left))
    right = jnp.where(wy < lax.axis_size("wy") - 1, right, jnp.zeros_like(right))
    wide = jnp.concatenate([left, centre, right], axis=2)
    summed = wide[:, 1 : rows + 1, 1 : cols + 1].astype(jnp.float32)
    for i in range(3):
        for j in range(3):
            part = wide[:, i : i + rows, j : j + cols].astype(jnp.float32)
            summed = summed + taps[i, j] * part
    return summed.astype(jnp.bfloat16)


def on_device(latent_cond, latent_uncond, qkv_weight, cond_pairs, guide_mask, shifts, kernel):
    _, frames, rows, cols, width_d = latent_cond.shape
    assert frames == 1 and rows == 2 * WIN
    heads = qkv_weight.shape[1] // (3 * HD)
    core = lax.axis_index("core")
    shift_rows, shift_cols = shifts[0, 0], shifts[0, 1]
    own_flag = guide_mask[0]
    flags = ordered(core, own_flag, cyc(own_flag, "core", 1), 0)
    info = jnp.concatenate([shifts[0, 1:], flags])
    firsts = [sum(CHUNKS[:i]) for i in range(len(CHUNKS))]
    weights = [gathered_weight(qkv_weight, heads, f, n) for f, n in zip(firsts, CHUNKS)]
    tokens = shifted_tokens(latent_cond[0, 0], latent_uncond[0, 0], shift_rows, shift_cols)
    tokens = tokens.reshape(-1, width_d)
    far = gathered_pairs(cond_pairs[0], heads)
    parts, others = [], []
    for first, count, weight in zip(firsts, CHUNKS, weights):
        projected = jnp.dot(tokens, weight, preferred_element_type=jnp.float32)
        projected = projected.astype(jnp.bfloat16)
        attended = attend(info, projected, far, first, count, 2 * cols)
        attended = attended.reshape(2, rows, 2 * cols, count * HD)
        taps = lax.dynamic_slice_in_dim(
            kernel, (core * (heads // 2) + first) * HD, count * HD, axis=2
        )
        part = refined_part(attended, taps, shift_rows, shift_cols)
        low, high = part[:, :, :cols], part[:, :, cols:]
        parts.append(jnp.where(core == 0, low, high))
        others.append(cyc(jnp.where(core == 0, high, low), "core", 1))
    out = ordered(core, jnp.concatenate(parts, -1), jnp.concatenate(others, -1), -1)
    return out[None, :, None]


def solution(mesh):
    clips, has, was = (mesh.shape[a] for a in ("clip", "ha", "wa"))
    split = Mesh(mesh.devices.reshape(clips, has, was // 2, 2), ("clip", "ha", "wy", "core"))
    wa = ("wy", "core")
    placed = (
        P("clip", None, "ha", wa, None),
        P("clip", None, "ha", wa, None),
        P(("clip", "ha") + wa, None),
        P("clip", None, ("ha",) + wa, None),
        P("clip", ("ha",) + wa),
        P("clip", None),
        P(),
    )
    return jax.shard_map(
        on_device,
        mesh=split,
        in_specs=placed,
        out_specs=P("clip", None, None, "ha", wa, None),
        check_vma=False,
    )
```

```python
import functools
import math

import jax
import jax.numpy as jnp
from jax import lax
from jax.experimental import pallas as pl
from jax.experimental.pallas import tpu as pltpu
from jax.sharding import Mesh
from jax.sharding import PartitionSpec as P


HD = 128
WIN = 8
RIM = WIN // 2
CHUNKS = (3, 2)


def cyc(x, axis, step):
    count = lax.axis_size(axis)
    return lax.ppermute(x, axis, [(i, (i + step) % count) for i in range(count)])


def ordered(flag, mine, other, axis):
    first = jnp.where(flag == 0, mine, other)
    second = jnp.where(flag == 0, other, mine)
    return jnp.concatenate([first, second], axis=axis)


def halves_kernel(core_ref, w_ref, mine_ref, other_ref, *, heads, chunks):
    half = heads // 2
    for ref, core in ((mine_ref, core_ref[0]), (other_ref, 1 - core_ref[0])):
        first, at = 0, 0
        for count in chunks:
            for kind in range(ref.shape[1] // (half * HD)):
                start = pl.multiple_of((kind * heads + core * half + first) * HD, HD)
                ref[:, at : at + count * HD] = w_ref[:, pl.ds(start, count * HD)]
                at += count * HD
            first += count


def core_halves(block, heads, chunks):
    rows, cols = block.shape
    half = jax.ShapeDtypeStruct((rows, cols // 2), block.dtype)
    core = lax.axis_index("core").reshape(1)
    return pl.pallas_call(
        functools.partial(halves_kernel, heads=heads, chunks=chunks),
        in_specs=[
            pl.BlockSpec(memory_space=pltpu.SMEM),
            pl.BlockSpec(memory_space=pltpu.VMEM),
        ],
        out_specs=[pl.BlockSpec(memory_space=pltpu.VMEM)] * 2,
        out_shape=[half, half],
        cost_estimate=pl.CostEstimate(flops=0, transcendentals=0, bytes_accessed=4 * block.size),
    )(core, block)


def along_line(block, axis):
    count = lax.axis_size(axis)
    if count != 4:
        near = [cyc(block, axis, d) for d in range(1, count)]
        return near, near[-1]
    steps = {1: [(0, 1), (1, 2), (2, 3)], 2: [(i, (i + 2) % 4) for i in range(4)]}
    steps[3] = [(b, a) for a, b in steps[1]]
    got = {}
    for d, pairs in steps.items():
        got[d] = lax.ppermute(block, axis, pairs)
    passed = lax.ppermute(got[2], axis, [(1, 0), (2, 3)])
    place = lax.axis_index(axis)
    first = jnp.where(place == 0, passed, got[1])
    third = jnp.where(place == 3, passed, got[3])
    return [first, got[2], third], got[2]


def weight_pieces(block, tag, chips):
    side, has = block.shape[0], lax.axis_size("ha")
    if chips != (2, 2):
        full = lax.all_gather(block, ("clip", "ha", "wy"), axis=0, tiled=True)
        return [full], None, side, full[:1]
    near, early = along_line(block, "ha")
    x_own, y_own = cyc(block, "clip", 1), cyc(block, "wy", 1)
    rest = jnp.concatenate(near, axis=0)
    x_rest, y_rest = cyc(rest, "clip", 1), cyc(rest, "wy", 1)
    total = has * side
    mid = 0 if tag == "a" else rest.shape[0] // 2
    arrays = [block, rest, x_own, x_rest, y_own, y_rest, cyc(x_own, "wy", 1)]
    if mid:
        arrays.append(cyc(x_rest[:mid], "wy", 1))
    arrays.append(cyc(y_rest[mid:], "clip", 1))
    pieces = []

    def add(array, begin, end, other_clip, other_wy):
        row = begin
        while row < end:
            d, skip = divmod(row, side)
            stop = min(end, (d + 1) * side)
            pieces.append((array, row - begin, stop - row, other_clip, d, other_wy, skip))
            row = stop

    for k, (oc, oy) in enumerate(((0, 0), (1, 0), (0, 1))):
        add(2 * k, 0, side, oc, oy)
        add(2 * k + 1, side, total, oc, oy)
    add(6, 0, side, 1, 1)
    if mid:
        add(7, side, side + mid, 1, 1)
    add(len(arrays) - 1, side + mid, total, 1, 1)
    return arrays, pieces, side, early


def project_kernel(place, tok_ref, *refs, pieces, side, has):
    arrays, (out_ref, full, sems) = refs[:-3], refs[-3:]
    copies = []
    for k, (array, begin, count, other_clip, d, other_wy, skip) in enumerate(pieces):
        clip = 1 - place[0] if other_clip else place[0]
        wy = 1 - place[2] if other_wy else place[2]
        ha = lax.rem(place[1] + (has - d), has)
        at = pl.multiple_of(((clip * has + ha) * 2 + wy) * side + skip, 16)
        copies.append(
            pltpu.make_async_copy(
                arrays[array].at[pl.ds(begin, count)], full.at[pl.ds(at, count)], sems.at[k]
            )
        )
    for copy in copies:
        copy.start()
    for copy in copies:
        copy.wait()

    @pl.loop(0, tok_ref.shape[0] // 256)
    def _(step):
        rows = pl.ds(pl.multiple_of(step * 256, 256), 256)
        out_ref[rows, :] = jnp.dot(
            tok_ref[rows, :], full[...], preferred_element_type=jnp.float32
        ).astype(out_ref.dtype)


def project(place, tokens, arrays, pieces, side):
    rows, width = tokens.shape
    cols = arrays[0].shape[1]
    if pieces is None:
        return jnp.dot(tokens, arrays[0], preferred_element_type=jnp.float32).astype(tokens.dtype)
    vmem = pl.BlockSpec(memory_space=pltpu.VMEM)
    return pl.pallas_call(
        functools.partial(
            project_kernel, pieces=tuple(pieces), side=side, has=lax.axis_size("ha")
        ),
        in_specs=[pl.BlockSpec(memory_space=pltpu.SMEM), vmem]
        + [pl.BlockSpec(memory_space=pl.ANY)] * len(arrays),
        out_specs=vmem,
        out_shape=jax.ShapeDtypeStruct((rows, cols), jnp.bfloat16),
        scratch_shapes=[
            pltpu.VMEM((width, cols), jnp.bfloat16),
            pltpu.SemaphoreType.DMA((len(pieces),)),
        ],
        cost_estimate=pl.CostEstimate(
            flops=2 * rows * width * cols, transcendentals=0, bytes_accessed=2 * width * cols
        ),
    )(place, tokens, *arrays)


def gathered_pairs(pairs, heads):
    kinds, _, _ = pairs.shape
    block = jnp.concatenate([pairs[k] for k in range(kinds)], axis=1)
    mine, other = core_halves(block, heads, (heads // 2,))
    both = jnp.concatenate([mine, cyc(other, "core", 1)], axis=0)
    steps = range(1, lax.axis_size("wy"))
    both = jnp.concatenate([both] + [cyc(both, "wy", d) for d in steps], axis=0)
    return [both] + [cyc(both, "ha", d) for d in range(1, lax.axis_size("ha"))]


def attend_kernel(info, q_ref, k_ref, v_ref, *refs, width):
    far_refs, (out_ref, bias_ref) = refs[:-2], refs[-2:]
    count = len(far_refs) // 2
    far_keys = jnp.concatenate([ref[...] for ref in far_refs[:count]], axis=0)
    far_values = jnp.concatenate([ref[...] for ref in far_refs[count:]], axis=0)
    rate = math.log2(math.e) / math.sqrt(HD)
    tokens = bias_ref.shape[0]
    shift = info[0]

    def window(shape, axis):
        slot = lax.broadcasted_iota(jnp.int32, shape, axis) & (width - 1)
        return ((slot - shift) & (width - 1)) >> 3

    @pl.when(pl.program_id(0) == 0)
    def _():
        same = window((tokens, tokens), 0) == window((tokens, tokens), 1)
        bias_ref[...] = jnp.where(same, 0.0, -jnp.inf)

    def product(a, b):
        return lax.dot_general(
            a, b, (((1,), (1,)), ((), ())), preferred_element_type=jnp.float32
        )

    def weighted(exps, values):
        ones = jnp.ones_like(values)
        return jnp.dot(
            exps.astype(jnp.bfloat16),
            jnp.concatenate([values, ones], axis=1),
            preferred_element_type=jnp.float32,
        )

    for part in range(4):
        rows = slice(part * tokens, (part + 1) * tokens)
        q = q_ref[rows, :]
        near = product(q, k_ref[rows, :]) + bias_ref[...]
        top = jnp.max(near, axis=-1, keepdims=True)
        if part < 2:
            far = product(q, far_keys)
            top = jnp.maximum(top, jnp.max(far, axis=-1, keepdims=True))
        mixed = weighted(jnp.exp2((near - top) * rate), v_ref[rows, :])
        if part < 2:
            mixed = mixed + weighted(jnp.exp2((far - top) * rate), far_values)
        result = mixed[:, :HD] / mixed[:, HD:]
        if part >= 2:
            keep = jnp.where(window((tokens, 1), 0) < width // 16, info[1], info[2]) > 0
            result = jnp.where(keep, result, 0.0)
        out_ref[rows, :] = result.astype(out_ref.dtype)


def attend(info, projected, far, first, count, width):
    total = projected.shape[0]
    tokens = total // 4
    all_heads = far[0].shape[1] // (2 * HD)
    far_rows = sum(part.shape[0] for part in far)

    def near_spec(offset):
        return pl.BlockSpec((total, HD), lambda i, s: (0, offset + i))

    def far_specs(offset):
        def at(i, s):
            return 0, offset + first + i

        return [pl.BlockSpec((part.shape[0], HD), at) for part in far]

    keys = 2 * tokens + 2 * far_rows
    return pl.pallas_call(
        functools.partial(attend_kernel, width=width),
        grid_spec=pltpu.PrefetchScalarGridSpec(
            num_scalar_prefetch=1,
            grid=(count,),
            in_specs=[
                near_spec(0),
                near_spec(count),
                near_spec(2 * count),
            ]
            + far_specs(0)
            + far_specs(all_heads),
            out_specs=pl.BlockSpec((total, HD), lambda i, s: (0, i)),
            scratch_shapes=[pltpu.VMEM((tokens, tokens), jnp.float32)],
        ),
        out_shape=jax.ShapeDtypeStruct((total, count * HD), jnp.bfloat16),
        cost_estimate=pl.CostEstimate(
            flops=8 * count * tokens * keys * HD,
            transcendentals=2 * count * tokens * keys,
            bytes_accessed=8 * total * count * HD,
        ),
    )(info, projected, projected, projected, *far, *far)


def rows_kernel(info, mine_ref, other_ref, *refs):
    halves, (out_ref, sems) = (refs[:4], refs[4:8]), refs[8:]
    rows, cols = refs[0].shape[:2]
    rim = refs[2].shape[1]

    def copy(source, branch, row, half, sem):
        core = info[1] if half == 0 else 1 - info[1]
        at = pl.multiple_of(core * cols, cols)
        return pltpu.make_async_copy(source, out_ref.at[branch, row, pl.ds(at, cols)], sem)

    def each(row, act):
        start = info[0] + row
        for half, (cond, uncond, above, below) in enumerate(halves):
            for branch, own in enumerate((cond, uncond)):
                sem = sems.at[row, 2 * half + branch]

                @pl.when(start < 0)
                def _():
                    act(copy(above.at[branch, jnp.clip(start + rim, 0, rim - 1)], branch, row, half, sem))

                @pl.when(start >= rows)
                def _():
                    act(copy(below.at[branch, jnp.clip(start - rows, 0, rim - 1)], branch, row, half, sem))

                @pl.when((start >= 0) & (start < rows))
                def _():
                    act(copy(own.at[jnp.clip(start, 0, rows - 1)], branch, row, half, sem))

    @pl.loop(0, rows)
    def _(row):
        each(row, lambda copy: copy.start())

    shift = info[2]
    first = pl.multiple_of(jnp.where(shift > 0, 0, 2 * cols - WIN), WIN)
    own_edge = (shift > 0) == (info[1] == 0)

    @pl.loop(0, rows)
    def _(row):
        each(row, lambda copy: copy.wait())
        slot = lax.broadcasted_iota(jnp.int32, (WIN, out_ref.shape[3]), 0)
        taken = jnp.where(shift > 0, slot - shift, WIN + shift - 1 - slot) < 0
        for branch in range(2):
            edge = jnp.where(own_edge, mine_ref[branch, row], other_ref[branch, row])
            edge = edge.astype(jnp.float32)
            place = pl.ds(first, WIN)
            held = out_ref[branch, row, place].astype(jnp.float32)
            both = jnp.concatenate([edge, edge], axis=0)
            out_ref[branch, row, place] = jnp.where(taken, both, held).astype(out_ref.dtype)


def shifted_tokens(lat_cond, lat_uncond, shift_rows, shift_cols, after):
    core = lax.axis_index("core")
    rows, cols, width = lat_cond.shape
    pair = [lat_cond, lat_uncond]
    late = list(lax.optimization_barrier((lat_cond, lat_uncond, after))[:2])
    twin = [cyc(lat_cond, "core", 1), cyc(lat_uncond, "core", 1)]
    above = cyc(jnp.stack([x[rows - RIM :] for x in late]), "ha", 1)
    below = cyc(jnp.stack([x[:RIM] for x in late]), "ha", -1)
    halves = pair + [above, below]
    halves += twin + [cyc(above, "core", 1), cyc(below, "core", 1)]
    low = jnp.stack([x[:, :RIM] for x in late]), above[:, :, :RIM], below[:, :, :RIM]
    high = [jnp.stack([x[:, cols - RIM :] for x in late])]
    high += [above[:, :, cols - RIM :], below[:, :, cols - RIM :]]
    own, up, dn = (jnp.where(core == 0, a, b) for a, b in zip(low, high))
    tall = jnp.concatenate([up, own, dn], axis=1)
    edge = lax.dynamic_slice_in_dim(tall, RIM + shift_rows, rows, axis=1)
    mine = cyc(edge, "wy", 1)
    other = cyc(mine, "core", 1)
    return pl.pallas_call(
        rows_kernel,
        in_specs=[pl.BlockSpec(memory_space=pltpu.SMEM)]
        + [pl.BlockSpec(memory_space=pltpu.VMEM)] * 2
        + [pl.BlockSpec(memory_space=pl.ANY)] * len(halves),
        out_specs=pl.BlockSpec(memory_space=pltpu.VMEM),
        out_shape=jax.ShapeDtypeStruct((2, rows, 2 * cols, width), lat_cond.dtype),
        scratch_shapes=[pltpu.SemaphoreType.DMA((rows, 4))],
        cost_estimate=pl.CostEstimate(
            flops=0, transcendentals=0, bytes_accessed=16 * rows * cols * width
        ),
    )(jnp.stack([shift_rows, core, shift_cols]), mine, other, *halves)


def refined_part(attended, taps, shift_rows, shift_cols):
    _, rows, cols, _ = attended.shape
    rim = RIM + 1
    above = cyc(attended[:, rows - rim :], "ha", 1)
    below = cyc(attended[:, :rim], "ha", -1)
    tall = jnp.concatenate([above, attended, below], axis=1)
    tall = lax.dynamic_slice_in_dim(tall, RIM - shift_rows, rows + 2, axis=1)
    ha, wy = lax.axis_index("ha"), lax.axis_index("wy")
    row = lax.broadcasted_iota(jnp.int32, (1, rows + 2, 1, 1), 1)
    inside = ((row > 0) | (ha > 0)) & ((row < rows + 1) | (ha < lax.axis_size("ha") - 1))
    tall = jnp.where(inside, tall, jnp.zeros_like(tall))
    first, last = tall[:, :, :1], tall[:, :, cols - 1 :]
    sent = jnp.where(
        shift_cols >= 0,
        jnp.concatenate([tall[:, :, :RIM], last], axis=2),
        jnp.concatenate([tall[:, :, cols - RIM :], first], axis=2),
    )
    got = cyc(sent, "wy", 1)
    blank = jnp.zeros(tall.shape[:2] + (cols - 2 * RIM,) + tall.shape[3:], tall.dtype)
    spread = jnp.concatenate([got[:, :, :RIM], blank, got[:, :, :RIM]], axis=2)
    slot = lax.broadcasted_iota(jnp.int32, (1, 1, cols, 1), 2)
    centre = jnp.where((slot < shift_cols) | (slot >= cols + shift_cols), spread, tall)
    left = jnp.where(shift_cols < 0, last, got[:, :, RIM:])
    right = jnp.where(
        shift_cols > 0, first, jnp.where(shift_cols < 0, got[:, :, RIM:], got[:, :, :1])
    )
    left = jnp.where(wy > 0, left, jnp.zeros_like(left))
    right = jnp.where(wy < lax.axis_size("wy") - 1, right, jnp.zeros_like(right))
    wide = jnp.concatenate([left, centre, right], axis=2)
    summed = wide[:, 1 : rows + 1, 1 : cols + 1].astype(jnp.float32)
    for i in range(3):
        for j in range(3):
            part = wide[:, i : i + rows, j : j + cols].astype(jnp.float32)
            summed = summed + taps[i, j] * part
    return summed.astype(jnp.bfloat16)


def on_device(latent_cond, latent_uncond, qkv_weight, cond_pairs, guide_mask, shifts, kernel):
    _, frames, rows, cols, width_d = latent_cond.shape
    assert frames == 1 and rows == 2 * WIN
    heads = qkv_weight.shape[1] // (3 * HD)
    core = lax.axis_index("core")
    shift_rows, shift_cols = shifts[0, 0], shifts[0, 1]
    own_flag = guide_mask[0]
    flags = ordered(core, own_flag, cyc(own_flag, "core", 1), 0)
    info = jnp.concatenate([shifts[0, 1:], flags])
    place = jnp.stack([lax.axis_index(a) for a in ("clip", "ha", "wy")])
    mine, other = core_halves(qkv_weight, heads, CHUNKS)
    block = ordered(core, mine, cyc(other, "core", 1), 0)
    chips = (lax.axis_size("clip"), lax.axis_size("wy"))
    firsts = [sum(CHUNKS[:i]) for i in range(len(CHUNKS))]
    tags = "abcde"[: len(CHUNKS)]
    held = (block, latent_cond, latent_uncond, cond_pairs)
    block, latent_cond, latent_uncond, cond_pairs = lax.optimization_barrier(held)
    weights = []
    for tag, first, count in zip(tags, firsts, CHUNKS):
        columns = block[:, 3 * first * HD : 3 * (first + count) * HD]
        weights.append(weight_pieces(columns, tag, chips))
    tokens = shifted_tokens(
        latent_cond[0, 0], latent_uncond[0, 0], shift_rows, shift_cols, weights[0][3]
    )
    tokens = tokens.reshape(-1, width_d)
    far = gathered_pairs(cond_pairs[0], heads)
    parts, others = [], []
    for tag, first, count, weight in zip(tags, firsts, CHUNKS, weights):
        projected = project(place, tokens, *weight[:3])
        attended = attend(info, projected, far, first, count, 2 * cols)
        attended = attended.reshape(2, rows, 2 * cols, count * HD)
        taps = lax.dynamic_slice_in_dim(
            kernel, (core * (heads // 2) + first) * HD, count * HD, axis=2
        )
        part = refined_part(attended, taps, shift_rows, shift_cols)
        low, high = part[:, :, :cols], part[:, :, cols:]
        parts.append(jnp.where(core == 0, low, high))
        others.append(cyc(jnp.where(core == 0, high, low), "core", 1))
    out = ordered(core, jnp.concatenate(parts, -1), jnp.concatenate(others, -1), -1)
    return out[None, :, None]


def solution(mesh):
    clips, has, was = (mesh.shape[a] for a in ("clip", "ha", "wa"))
    split = Mesh(mesh.devices.reshape(clips, has, was // 2, 2), ("clip", "ha", "wy", "core"))
    wa = ("wy", "core")
    placed = (
        P("clip", None, "ha", wa, None),
        P("clip", None, "ha", wa, None),
        P(("clip", "ha") + wa, None),
        P("clip", None, ("ha",) + wa, None),
        P("clip", ("ha",) + wa),
        P("clip", None),
        P(),
    )

    return jax.shard_map(
        on_device,
        mesh=split,
        in_specs=placed,
        out_specs=P("clip", None, None, "ha", wa, None),
        check_vma=False,
    )
```

```python
import functools
import math

import jax
import jax.numpy as jnp
from jax import lax
from jax.experimental import pallas as pl
from jax.experimental.pallas import tpu as pltpu
from jax.sharding import Mesh
from jax.sharding import PartitionSpec as P


HD = 128
WIN = 8
RIM = WIN // 2
CHUNKS = (3, 2)


def cyc(x, axis, step):
    count = lax.axis_size(axis)
    return lax.ppermute(x, axis, [(i, (i + step) % count) for i in range(count)])


def ordered(flag, mine, other, axis):
    first = jnp.where(flag == 0, mine, other)
    second = jnp.where(flag == 0, other, mine)
    return jnp.concatenate([first, second], axis=axis)


def halves_kernel(w_ref, mine_ref, other_ref, *, heads, chunks):
    half = heads // 2
    own = lax.axis_index("core")
    for ref, core in ((mine_ref, own), (other_ref, 1 - own)):
        first, at = 0, 0
        for count in chunks:
            for kind in range(ref.shape[1] // (half * HD)):
                start = pl.multiple_of((kind * heads + core * half + first) * HD, HD)
                ref[:, at : at + count * HD] = w_ref[:, pl.ds(start, count * HD)]
                at += count * HD
            first += count


def core_halves(block, heads, chunks):
    rows, cols = block.shape
    half = jax.ShapeDtypeStruct((rows, cols // 2), block.dtype)
    return pl.pallas_call(
        functools.partial(halves_kernel, heads=heads, chunks=chunks),
        in_specs=[pl.BlockSpec(memory_space=pltpu.VMEM)],
        out_specs=[pl.BlockSpec(memory_space=pltpu.VMEM)] * 2,
        out_shape=[half, half],
        cost_estimate=pl.CostEstimate(flops=0, transcendentals=0, bytes_accessed=4 * block.size),
    )(block)


def along_line(block, axis):
    count = lax.axis_size(axis)
    if count != 4:
        near = [cyc(block, axis, d) for d in range(1, count)]
        return near, near[-1]
    steps = {1: [(0, 1), (1, 2), (2, 3)], 2: [(i, (i + 2) % 4) for i in range(4)]}
    steps[3] = [(b, a) for a, b in steps[1]]
    got = {}
    for d, pairs in steps.items():
        got[d] = lax.ppermute(block, axis, pairs)
    passed = lax.ppermute(got[2], axis, [(1, 0), (2, 3)])
    place = lax.axis_index(axis)
    first = jnp.where(place == 0, passed, got[1])
    third = jnp.where(place == 3, passed, got[3])
    return [first, got[2], third], got[2]


def weight_pieces(block, tag, chips):
    side, has = block.shape[0], lax.axis_size("ha")
    if chips != (2, 2):
        full = lax.all_gather(block, ("clip", "ha", "wy"), axis=0, tiled=True)
        return [full], None, side, full[:1]
    near, early = along_line(block, "ha")
    x_own, y_own = cyc(block, "clip", 1), cyc(block, "wy", 1)
    rest = jnp.concatenate(near, axis=0)
    x_rest, y_rest = cyc(rest, "clip", 1), cyc(rest, "wy", 1)
    total = has * side
    mid = 0 if tag == "a" else rest.shape[0] // 2
    arrays = [block, rest, x_own, x_rest, y_own, y_rest, cyc(x_own, "wy", 1)]
    if mid:
        arrays.append(cyc(x_rest[:mid], "wy", 1))
    arrays.append(cyc(y_rest[mid:], "clip", 1))
    pieces = []

    def add(array, begin, end, other_clip, other_wy):
        row = begin
        while row < end:
            d, skip = divmod(row, side)
            stop = min(end, (d + 1) * side)
            pieces.append((array, row - begin, stop - row, other_clip, d, other_wy, skip))
            row = stop

    for k, (oc, oy) in enumerate(((0, 0), (1, 0), (0, 1))):
        add(2 * k, 0, side, oc, oy)
        add(2 * k + 1, side, total, oc, oy)
    add(6, 0, side, 1, 1)
    if mid:
        add(7, side, side + mid, 1, 1)
    add(len(arrays) - 1, side + mid, total, 1, 1)
    return arrays, pieces, side, early


def project_kernel(tok_ref, *refs, pieces, side, has):
    arrays, (out_ref, full, held, made, sems, tok_sems, out_sems) = refs[:-7], refs[-7:]
    place = [lax.axis_index(axis) for axis in ("clip", "ha", "wy")]
    copies = []
    for k, (array, begin, count, other_clip, d, other_wy, skip) in enumerate(pieces):
        clip = 1 - place[0] if other_clip else place[0]
        wy = 1 - place[2] if other_wy else place[2]
        ha = lax.rem(place[1] + (has - d), has)
        at = pl.multiple_of(((clip * has + ha) * 2 + wy) * side + skip, 16)
        copies.append(
            pltpu.make_async_copy(
                arrays[array].at[pl.ds(begin, count)], full.at[pl.ds(at, count)], sems.at[k]
            )
        )
    high = held.shape[1]
    tiles = held.shape[0]
    loads = [
        pltpu.make_async_copy(tok_ref.at[pl.ds(k * high, high)], held.at[k], tok_sems.at[k])
        for k in range(tiles)
    ]
    stores = [
        pltpu.make_async_copy(made.at[k], out_ref.at[pl.ds(k * high, high)], out_sems.at[k])
        for k in range(tiles)
    ]
    for copy in copies:
        copy.start()
    loads[0].start()
    for copy in copies:
        copy.wait()
    for k in range(tiles):
        loads[k].wait()
        if k == 0:
            for load in loads[1:]:
                load.start()
        made[k] = jnp.dot(held[k], full[...], preferred_element_type=jnp.float32).astype(
            made.dtype
        )
        stores[k].start()
    for store in stores:
        store.wait()


def project(tokens, arrays, pieces, side):
    rows, width = tokens.shape
    cols = arrays[0].shape[1]
    if pieces is None:
        return jnp.dot(tokens, arrays[0], preferred_element_type=jnp.float32).astype(tokens.dtype)
    hbm = pl.BlockSpec(memory_space=pl.ANY)
    tiles = 4
    return pl.pallas_call(
        functools.partial(
            project_kernel, pieces=tuple(pieces), side=side, has=lax.axis_size("ha")
        ),
        in_specs=[hbm]
        + [hbm] * len(arrays),
        out_specs=hbm,
        out_shape=jax.ShapeDtypeStruct((rows, cols), jnp.bfloat16),
        scratch_shapes=[
            pltpu.VMEM((width, cols), jnp.bfloat16),
            pltpu.VMEM((tiles, rows // tiles, width), jnp.bfloat16),
            pltpu.VMEM((tiles, rows // tiles, cols), jnp.bfloat16),
            pltpu.SemaphoreType.DMA((len(pieces),)),
            pltpu.SemaphoreType.DMA((tiles,)),
            pltpu.SemaphoreType.DMA((tiles,)),
        ],
        cost_estimate=pl.CostEstimate(
            flops=2 * rows * width * cols, transcendentals=0, bytes_accessed=2 * width * cols
        ),
    )(tokens, *arrays)


def gathered_pairs(pairs, heads):
    kinds, _, _ = pairs.shape
    block = jnp.concatenate([pairs[k] for k in range(kinds)], axis=1)
    mine, other = core_halves(block, heads, (heads // 2,))
    both = jnp.concatenate([mine, cyc(other, "core", 1)], axis=0)
    steps = range(1, lax.axis_size("wy"))
    both = jnp.concatenate([both] + [cyc(both, "wy", d) for d in steps], axis=0)
    return [both] + [cyc(both, "ha", d) for d in range(1, lax.axis_size("ha"))]


def attend_kernel(shifts_ref, own_ref, twin_ref, q_ref, k_ref, v_ref, *refs, width):
    far_refs, (out_ref, bias_ref) = refs[:-2], refs[-2:]
    count = len(far_refs) // 2
    far_keys = jnp.concatenate([ref[...] for ref in far_refs[:count]], axis=0)
    far_values = jnp.concatenate([ref[...] for ref in far_refs[count:]], axis=0)
    rate = math.log2(math.e) / math.sqrt(HD)
    tokens = bias_ref.shape[0]
    shift = shifts_ref[0, 1]
    first_core = lax.axis_index("core") == 0
    low = jnp.where(first_core, own_ref[0, 0], twin_ref[0, 0])
    high = jnp.where(first_core, twin_ref[0, 0], own_ref[0, 0])

    def window(shape, axis):
        slot = lax.broadcasted_iota(jnp.int32, shape, axis) & (width - 1)
        return ((slot - shift) & (width - 1)) >> 3

    @pl.when(pl.program_id(0) == 0)
    def _():
        same = window((tokens, tokens), 0) == window((tokens, tokens), 1)
        bias_ref[...] = jnp.where(same, 0.0, -jnp.inf)

    def product(a, b):
        return lax.dot_general(
            a, b, (((1,), (1,)), ((), ())), preferred_element_type=jnp.float32
        )

    def weighted(exps, values):
        ones = jnp.ones_like(values)
        return jnp.dot(
            exps.astype(jnp.bfloat16),
            jnp.concatenate([values, ones], axis=1),
            preferred_element_type=jnp.float32,
        )

    for part in range(4):
        rows = slice(part * tokens, (part + 1) * tokens)
        q = q_ref[rows, :]
        near = product(q, k_ref[rows, :]) + bias_ref[...]
        top = jnp.max(near, axis=-1, keepdims=True)
        if part < 2:
            far = product(q, far_keys)
            top = jnp.maximum(top, jnp.max(far, axis=-1, keepdims=True))
        mixed = weighted(jnp.exp2((near - top) * rate), v_ref[rows, :])
        if part < 2:
            mixed = mixed + weighted(jnp.exp2((far - top) * rate), far_values)
        result = mixed[:, :HD] / mixed[:, HD:]
        if part >= 2:
            keep = jnp.where(window((tokens, 1), 0) < width // 16, low, high) > 0
            result = jnp.where(keep, result, 0.0)
        out_ref[rows, :] = result.astype(out_ref.dtype)


def attend(info, projected, far, first, count, width):
    total = projected.shape[0]
    tokens = total // 4
    all_heads = far[0].shape[1] // (2 * HD)
    far_rows = sum(part.shape[0] for part in far)

    def near_spec(offset):
        return pl.BlockSpec((total, HD), lambda i, *s: (0, offset + i))

    def far_specs(offset):
        def at(i, *s):
            return 0, offset + first + i

        return [pl.BlockSpec((part.shape[0], HD), at) for part in far]

    keys = 2 * tokens + 2 * far_rows
    return pl.pallas_call(
        functools.partial(attend_kernel, width=width),
        grid_spec=pltpu.PrefetchScalarGridSpec(
            num_scalar_prefetch=3,
            grid=(count,),
            in_specs=[
                near_spec(0),
                near_spec(count),
                near_spec(2 * count),
            ]
            + far_specs(0)
            + far_specs(all_heads),
            out_specs=pl.BlockSpec((total, HD), lambda i, *s: (0, i)),
            scratch_shapes=[pltpu.VMEM((tokens, tokens), jnp.float32)],
        ),
        out_shape=jax.ShapeDtypeStruct((total, count * HD), jnp.bfloat16),
        cost_estimate=pl.CostEstimate(
            flops=8 * count * tokens * keys * HD,
            transcendentals=2 * count * tokens * keys,
            bytes_accessed=8 * total * count * HD,
        ),
    )(*info, projected, projected, projected, *far, *far)


def rows_kernel(shifts_ref, mine_ref, other_ref, *refs):
    halves, (out_ref, sems) = (refs[:4], refs[4:8]), refs[-2:]
    info = shifts_ref[0, 0], lax.axis_index("core"), shifts_ref[0, 1]
    rows, cols = refs[0].shape[:2]
    rim = refs[2].shape[1]

    def copy(source, branch, row, half, sem):
        core = info[1] if half == 0 else 1 - info[1]
        at = pl.multiple_of(core * cols, cols)
        return pltpu.make_async_copy(source, out_ref.at[branch, row, pl.ds(at, cols)], sem)

    def each(row, act):
        start = info[0] + row
        for half, (cond, uncond, above, below) in enumerate(halves):
            for branch, own in enumerate((cond, uncond)):
                sem = sems.at[row, 2 * half + branch]

                @pl.when(start < 0)
                def _():
                    act(copy(above.at[branch, jnp.clip(start + rim, 0, rim - 1)], branch, row, half, sem))

                @pl.when(start >= rows)
                def _():
                    act(copy(below.at[branch, jnp.clip(start - rows, 0, rim - 1)], branch, row, half, sem))

                @pl.when((start >= 0) & (start < rows))
                def _():
                    act(copy(own.at[jnp.clip(start, 0, rows - 1)], branch, row, half, sem))

    @pl.loop(0, rows)
    def _(row):
        each(row, lambda copy: copy.start())

    shift = info[2]
    first = pl.multiple_of(jnp.where(shift > 0, 0, 2 * cols - WIN), WIN)
    own_edge = (shift > 0) == (info[1] == 0)

    @pl.loop(0, rows)
    def _(row):
        each(row, lambda copy: copy.wait())
        slot = lax.broadcasted_iota(jnp.int32, (WIN, out_ref.shape[3]), 0)
        taken = jnp.where(shift > 0, slot - shift, WIN + shift - 1 - slot) < 0
        for branch in range(2):
            edge = jnp.where(own_edge, mine_ref[branch, row], other_ref[branch, row])
            edge = edge.astype(jnp.float32)
            place = pl.ds(first, WIN)
            held = out_ref[branch, row, place].astype(jnp.float32)
            both = jnp.concatenate([edge, edge], axis=0)
            out_ref[branch, row, place] = jnp.where(taken, both, held).astype(out_ref.dtype)


def shifted_tokens(lat_cond, lat_uncond, shifts, after, taps):
    core = lax.axis_index("core")
    rows, cols, width = lat_cond.shape
    pair = [lat_cond, lat_uncond]
    shift_rows = shifts[0, 0]
    late = list(lax.optimization_barrier((lat_cond, lat_uncond, after))[:2])
    twin = [cyc(lat_cond, "core", 1), cyc(lat_uncond, "core", 1)]
    above = cyc(jnp.stack([x[rows - RIM :] for x in late]), "ha", 1)
    below = cyc(jnp.stack([x[:RIM] for x in late]), "ha", -1)
    halves = pair + [above, below]
    halves += twin + [cyc(above, "core", 1), cyc(below, "core", 1)]
    low = jnp.stack([x[:, :RIM] for x in late]), above[:, :, :RIM], below[:, :, :RIM]
    high = [jnp.stack([x[:, cols - RIM :] for x in late])]
    high += [above[:, :, cols - RIM :], below[:, :, cols - RIM :]]
    own, up, dn = (jnp.where(core == 0, a, b) for a, b in zip(low, high))
    tall = jnp.concatenate([up, own, dn], axis=1)
    start = (RIM + shift_rows).astype(jnp.uint32)
    edge = lax.dynamic_slice_in_dim(tall, start, rows, axis=1)
    mine = cyc(edge, "wy", 1)
    other = cyc(mine, "core", 1)
    return pl.pallas_call(
        rows_kernel,
        in_specs=[pl.BlockSpec(memory_space=pltpu.SMEM)]
        + [pl.BlockSpec(memory_space=pltpu.VMEM)] * 2
        + [pl.BlockSpec(memory_space=pl.ANY)] * (len(halves) + len(taps)),
        out_specs=pl.BlockSpec(memory_space=pltpu.VMEM),
        out_shape=jax.ShapeDtypeStruct((2, rows, 2 * cols, width), lat_cond.dtype),
        scratch_shapes=[pltpu.SemaphoreType.DMA((rows, 4))],
        cost_estimate=pl.CostEstimate(
            flops=0, transcendentals=0, bytes_accessed=16 * rows * cols * width
        ),
    )(shifts, mine, other, *halves, *taps)


def refined_part(attended, taps, shift_rows, shift_cols):
    _, rows, cols, _ = attended.shape
    rim = RIM + 1
    above = cyc(attended[:, rows - rim :], "ha", 1)
    below = cyc(attended[:, :rim], "ha", -1)
    tall = jnp.concatenate([above, attended, below], axis=1)
    start = (RIM - shift_rows).astype(jnp.uint32)
    tall = lax.dynamic_slice_in_dim(tall, start, rows + 2, axis=1)
    ha, wy = lax.axis_index("ha"), lax.axis_index("wy")
    row = lax.broadcasted_iota(jnp.int32, (1, rows + 2, 1, 1), 1)
    inside = ((row > 0) | (ha > 0)) & ((row < rows + 1) | (ha < lax.axis_size("ha") - 1))
    tall = jnp.where(inside, tall, jnp.zeros_like(tall))
    first, last = tall[:, :, :1], tall[:, :, cols - 1 :]
    sent = jnp.where(
        shift_cols >= 0,
        jnp.concatenate([tall[:, :, :RIM], last], axis=2),
        jnp.concatenate([tall[:, :, cols - RIM :], first], axis=2),
    )
    got = cyc(sent, "wy", 1)
    blank = jnp.zeros(tall.shape[:2] + (cols - 2 * RIM,) + tall.shape[3:], tall.dtype)
    spread = jnp.concatenate([got[:, :, :RIM], blank, got[:, :, :RIM]], axis=2)
    slot = lax.broadcasted_iota(jnp.int32, (1, 1, cols, 1), 2)
    centre = jnp.where((slot < shift_cols) | (slot >= cols + shift_cols), spread, tall)
    left = jnp.where(shift_cols < 0, last, got[:, :, RIM:])
    right = jnp.where(
        shift_cols > 0, first, jnp.where(shift_cols < 0, got[:, :, RIM:], got[:, :, :1])
    )
    left = jnp.where(wy > 0, left, jnp.zeros_like(left))
    right = jnp.where(wy < lax.axis_size("wy") - 1, right, jnp.zeros_like(right))
    wide = jnp.concatenate([left, centre, right], axis=2)
    summed = wide[:, 1 : rows + 1, 1 : cols + 1].astype(jnp.float32)
    for i in range(3):
        for j in range(3):
            part = wide[:, i : i + rows, j : j + cols].astype(jnp.float32)
            summed = summed + taps[i, j] * part
    return summed.astype(jnp.bfloat16)


def on_device(latent_cond, latent_uncond, qkv_weight, cond_pairs, guide_mask, shifts, kernel):
    _, frames, rows, cols, width_d = latent_cond.shape
    assert frames == 1 and rows == 2 * WIN
    heads = qkv_weight.shape[1] // (3 * HD)
    core = lax.axis_index("core")
    shift_rows, shift_cols = shifts[0, 0], shifts[0, 1]
    info = shifts, guide_mask, cyc(guide_mask, "core", 1)
    mine, other = core_halves(qkv_weight, heads, CHUNKS)
    block = ordered(core, mine, cyc(other, "core", 1), 0)
    chips = (lax.axis_size("clip"), lax.axis_size("wy"))
    firsts = [sum(CHUNKS[:i]) for i in range(len(CHUNKS))]
    tags = "abcde"[: len(CHUNKS)]
    held = (block, latent_cond, latent_uncond, cond_pairs)
    block, latent_cond, latent_uncond, cond_pairs = lax.optimization_barrier(held)
    weights = []
    for tag, first, count in zip(tags, firsts, CHUNKS):
        columns = block[:, 3 * first * HD : 3 * (first + count) * HD]
        weights.append(weight_pieces(columns, tag, chips))
    taps = []
    for first, count in zip(firsts, CHUNKS):
        at = ((core * (heads // 2) + first) * HD).astype(jnp.uint32)
        taps.append(lax.dynamic_slice_in_dim(kernel, at, count * HD, axis=2))
    tokens = shifted_tokens(
        latent_cond[0, 0], latent_uncond[0, 0], shifts, weights[0][3], taps
    )
    tokens = tokens.reshape(-1, width_d)
    far = gathered_pairs(cond_pairs[0], heads)
    parts, others = [], []
    for tag, first, count, weight, part_taps in zip(tags, firsts, CHUNKS, weights, taps):
        projected = project(tokens, *weight[:3])
        attended = attend(info, projected, far, first, count, 2 * cols)
        attended = attended.reshape(2, rows, 2 * cols, count * HD)
        part = refined_part(attended, part_taps, shift_rows, shift_cols)
        low, high = part[:, :, :cols], part[:, :, cols:]
        parts.append(jnp.where(core == 0, low, high))
        others.append(cyc(jnp.where(core == 0, high, low), "core", 1))
    out = ordered(core, jnp.concatenate(parts, -1), jnp.concatenate(others, -1), -1)
    return out[None, :, None]


def solution(mesh):
    clips, has, was = (mesh.shape[a] for a in ("clip", "ha", "wa"))
    split = Mesh(mesh.devices.reshape(clips, has, was // 2, 2), ("clip", "ha", "wy", "core"))
    wa = ("wy", "core")
    placed = (
        P("clip", None, "ha", wa, None),
        P("clip", None, "ha", wa, None),
        P(("clip", "ha") + wa, None),
        P("clip", None, ("ha",) + wa, None),
        P("clip", ("ha",) + wa),
        P("clip", None),
        P(),
    )

    return jax.shard_map(
        on_device,
        mesh=split,
        in_specs=placed,
        out_specs=P("clip", None, None, "ha", wa, None),
        check_vma=False,
    )
```

```python
import functools
import math

import jax
import jax.numpy as jnp
from jax import lax
from jax.experimental import pallas as pl
from jax.experimental.pallas import tpu as pltpu
from jax.sharding import Mesh
from jax.sharding import PartitionSpec as P


HD = 128
WIN = 8
RIM = WIN // 2
CHUNKS = (3, 2)


def cyc(x, axis, step):
    count = lax.axis_size(axis)
    return lax.ppermute(x, axis, [(i, (i + step) % count) for i in range(count)])


def ordered(flag, mine, other, axis):
    first = jnp.where(flag == 0, mine, other)
    second = jnp.where(flag == 0, other, mine)
    return jnp.concatenate([first, second], axis=axis)


def halves_kernel(w_ref, mine_ref, other_ref, *, heads, chunks):
    half = heads // 2
    own = lax.axis_index("core")
    for ref, core in ((mine_ref, own), (other_ref, 1 - own)):
        first, at = 0, 0
        for count in chunks:
            for kind in range(ref.shape[1] // (half * HD)):
                start = pl.multiple_of((kind * heads + core * half + first) * HD, HD)
                ref[:, at : at + count * HD] = w_ref[:, pl.ds(start, count * HD)]
                at += count * HD
            first += count


def core_halves(block, heads, chunks):
    rows, cols = block.shape
    half = jax.ShapeDtypeStruct((rows, cols // 2), block.dtype)
    return pl.pallas_call(
        functools.partial(halves_kernel, heads=heads, chunks=chunks),
        in_specs=[pl.BlockSpec(memory_space=pltpu.VMEM)],
        out_specs=[pl.BlockSpec(memory_space=pltpu.VMEM)] * 2,
        out_shape=[half, half],
        cost_estimate=pl.CostEstimate(flops=0, transcendentals=0, bytes_accessed=4 * block.size),
    )(block)


def along_line(block, axis):
    count = lax.axis_size(axis)
    if count != 4:
        near = [cyc(block, axis, d) for d in range(1, count)]
        return near, near[-1]
    steps = {1: [(0, 1), (1, 2), (2, 3)], 2: [(i, (i + 2) % 4) for i in range(4)]}
    steps[3] = [(b, a) for a, b in steps[1]]
    got = {}
    for d, pairs in steps.items():
        got[d] = lax.ppermute(block, axis, pairs)
    passed = lax.ppermute(got[2], axis, [(1, 0), (2, 3)])
    place = lax.axis_index(axis)
    first = jnp.where(place == 0, passed, got[1])
    third = jnp.where(place == 3, passed, got[3])
    return [first, got[2], third], got[2]


def weight_pieces(block, tag, chips):
    side, has = block.shape[0], lax.axis_size("ha")
    if chips != (2, 2):
        full = lax.all_gather(block, ("clip", "ha", "wy"), axis=0, tiled=True)
        return [full], None, side, full[:1]
    near, early = along_line(block, "ha")
    x_own, y_own = cyc(block, "clip", 1), cyc(block, "wy", 1)
    rest = jnp.concatenate(near, axis=0)
    x_rest, y_rest = cyc(rest, "clip", 1), cyc(rest, "wy", 1)
    total = has * side
    mid = 0 if tag == "a" else rest.shape[0] // 2
    arrays = [block, rest, x_own, x_rest, y_own, y_rest, cyc(x_own, "wy", 1)]
    if mid:
        arrays.append(cyc(x_rest[:mid], "wy", 1))
    arrays.append(cyc(y_rest[mid:], "clip", 1))
    pieces = []

    def add(array, begin, end, other_clip, other_wy):
        row = begin
        while row < end:
            d, skip = divmod(row, side)
            stop = min(end, (d + 1) * side)
            pieces.append((array, row - begin, stop - row, other_clip, d, other_wy, skip))
            row = stop

    for k, (oc, oy) in enumerate(((0, 0), (1, 0), (0, 1))):
        add(2 * k, 0, side, oc, oy)
        add(2 * k + 1, side, total, oc, oy)
    add(6, 0, side, 1, 1)
    if mid:
        add(7, side, side + mid, 1, 1)
    add(len(arrays) - 1, side + mid, total, 1, 1)
    return arrays, pieces, side, early


def project_kernel(tok_ref, *refs, pieces, side, has):
    arrays, (out_ref, full, held, made, sems, tok_sems, out_sems) = refs[:-7], refs[-7:]
    place = [lax.axis_index(axis) for axis in ("clip", "ha", "wy")]
    copies = []
    for k, (array, begin, count, other_clip, d, other_wy, skip) in enumerate(pieces):
        clip = 1 - place[0] if other_clip else place[0]
        wy = 1 - place[2] if other_wy else place[2]
        ha = lax.rem(place[1] + (has - d), has)
        at = pl.multiple_of(((clip * has + ha) * 2 + wy) * side + skip, 16)
        copies.append(
            pltpu.make_async_copy(
                arrays[array].at[pl.ds(begin, count)], full.at[pl.ds(at, count)], sems.at[k]
            )
        )
    high = held.shape[1]
    tiles = held.shape[0]
    loads = [
        pltpu.make_async_copy(tok_ref.at[pl.ds(k * high, high)], held.at[k], tok_sems.at[k])
        for k in range(tiles)
    ]
    stores = [
        pltpu.make_async_copy(made.at[k], out_ref.at[pl.ds(k * high, high)], out_sems.at[k])
        for k in range(tiles)
    ]
    for copy in copies:
        copy.start()
    loads[0].start()
    for copy in copies:
        copy.wait()
    for k in range(tiles):
        loads[k].wait()
        if k == 0:
            for load in loads[1:]:
                load.start()
        made[k] = jnp.dot(held[k], full[...], preferred_element_type=jnp.float32).astype(
            made.dtype
        )
        stores[k].start()
    for store in stores:
        store.wait()


def project(tokens, arrays, pieces, side):
    rows, width = tokens.shape
    cols = arrays[0].shape[1]
    if pieces is None:
        return jnp.dot(tokens, arrays[0], preferred_element_type=jnp.float32).astype(tokens.dtype)
    hbm = pl.BlockSpec(memory_space=pl.ANY)
    tiles = 4
    return pl.pallas_call(
        functools.partial(
            project_kernel, pieces=tuple(pieces), side=side, has=lax.axis_size("ha")
        ),
        in_specs=[hbm]
        + [hbm] * len(arrays),
        out_specs=hbm,
        out_shape=jax.ShapeDtypeStruct((rows, cols), jnp.bfloat16),
        scratch_shapes=[
            pltpu.VMEM((width, cols), jnp.bfloat16),
            pltpu.VMEM((tiles, rows // tiles, width), jnp.bfloat16),
            pltpu.VMEM((tiles, rows // tiles, cols), jnp.bfloat16),
            pltpu.SemaphoreType.DMA((len(pieces),)),
            pltpu.SemaphoreType.DMA((tiles,)),
            pltpu.SemaphoreType.DMA((tiles,)),
        ],
        cost_estimate=pl.CostEstimate(
            flops=2 * rows * width * cols, transcendentals=0, bytes_accessed=2 * width * cols
        ),
    )(tokens, *arrays)


def gathered_pairs(pairs, heads):
    kinds, _, _ = pairs.shape
    block = jnp.concatenate([pairs[k] for k in range(kinds)], axis=1)
    mine, other = core_halves(block, heads, (heads // 2,))
    both = jnp.concatenate([mine, cyc(other, "core", 1)], axis=0)
    steps = range(1, lax.axis_size("wy"))
    both = jnp.concatenate([both] + [cyc(both, "wy", d) for d in steps], axis=0)
    return [both] + [cyc(both, "ha", d) for d in range(1, lax.axis_size("ha"))]


def attend_kernel(shifts_ref, own_ref, twin_ref, q_ref, k_ref, v_ref, *refs, width):
    far_refs, (out_ref, bias_ref) = refs[:-2], refs[-2:]
    count = len(far_refs) // 2
    far_keys = jnp.concatenate([ref[...] for ref in far_refs[:count]], axis=0)
    far_values = jnp.concatenate([ref[...] for ref in far_refs[count:]], axis=0)
    rate = math.log2(math.e) / math.sqrt(HD)
    tokens = bias_ref.shape[0]
    shift = shifts_ref[0, 1]
    first_core = lax.axis_index("core") == 0
    low = jnp.where(first_core, own_ref[0, 0], twin_ref[0, 0])
    high = jnp.where(first_core, twin_ref[0, 0], own_ref[0, 0])

    def window(shape, axis):
        slot = lax.broadcasted_iota(jnp.int32, shape, axis) & (width - 1)
        return ((slot - shift) & (width - 1)) >> 3

    @pl.when(pl.program_id(0) == 0)
    def _():
        same = window((tokens, tokens), 0) == window((tokens, tokens), 1)
        bias_ref[...] = jnp.where(same, 0.0, -jnp.inf)

    def product(a, b):
        return lax.dot_general(
            a, b, (((1,), (1,)), ((), ())), preferred_element_type=jnp.float32
        )

    def weighted(exps, values):
        ones = jnp.ones_like(values)
        return jnp.dot(
            exps.astype(jnp.bfloat16),
            jnp.concatenate([values, ones], axis=1),
            preferred_element_type=jnp.float32,
        )

    for part in range(4):
        rows = slice(part * tokens, (part + 1) * tokens)
        q = q_ref[rows, :]
        near = product(q, k_ref[rows, :]) + bias_ref[...]
        values = v_ref[rows, :]
        if part < 2:
            near = jnp.concatenate([near, product(q, far_keys)], axis=1)
            values = jnp.concatenate([values, far_values], axis=0)
        top = jnp.max(near, axis=-1, keepdims=True)
        mixed = weighted(jnp.exp2((near - top) * rate), values)
        result = mixed[:, :HD] / mixed[:, HD:]
        if part >= 2:
            keep = jnp.where(window((tokens, 1), 0) < width // 16, low, high) > 0
            result = jnp.where(keep, result, 0.0)
        out_ref[rows, :] = result.astype(out_ref.dtype)


def attend(info, projected, far, first, count, width):
    total = projected.shape[0]
    tokens = total // 4
    all_heads = far[0].shape[1] // (2 * HD)
    far_rows = sum(part.shape[0] for part in far)

    def near_spec(offset):
        return pl.BlockSpec((total, HD), lambda i, *s: (0, offset + i))

    def far_specs(offset):
        def at(i, *s):
            return 0, offset + first + i

        return [pl.BlockSpec((part.shape[0], HD), at) for part in far]

    keys = 2 * tokens + 2 * far_rows
    return pl.pallas_call(
        functools.partial(attend_kernel, width=width),
        grid_spec=pltpu.PrefetchScalarGridSpec(
            num_scalar_prefetch=3,
            grid=(count,),
            in_specs=[
                near_spec(0),
                near_spec(count),
                near_spec(2 * count),
            ]
            + far_specs(0)
            + far_specs(all_heads),
            out_specs=pl.BlockSpec((total, HD), lambda i, *s: (0, i)),
            scratch_shapes=[pltpu.VMEM((tokens, tokens), jnp.float32)],
        ),
        out_shape=jax.ShapeDtypeStruct((total, count * HD), jnp.bfloat16),
        cost_estimate=pl.CostEstimate(
            flops=8 * count * tokens * keys * HD,
            transcendentals=2 * count * tokens * keys,
            bytes_accessed=8 * total * count * HD,
        ),
    )(*info, projected, projected, projected, *far, *far)


def rows_kernel(shifts_ref, mine_ref, other_ref, *refs):
    halves, (out_ref, sems) = (refs[:4], refs[4:8]), refs[-2:]
    info = shifts_ref[0, 0], lax.axis_index("core"), shifts_ref[0, 1]
    rows, cols = refs[0].shape[:2]
    rim = refs[2].shape[1]

    def copy(source, branch, row, half, sem):
        core = info[1] if half == 0 else 1 - info[1]
        at = pl.multiple_of(core * cols, cols)
        return pltpu.make_async_copy(source, out_ref.at[branch, row, pl.ds(at, cols)], sem)

    def each(row, act):
        start = info[0] + row
        for half, (cond, uncond, above, below) in enumerate(halves):
            for branch, own in enumerate((cond, uncond)):
                sem = sems.at[row, 2 * half + branch]

                @pl.when(start < 0)
                def _():
                    act(copy(above.at[branch, jnp.clip(start + rim, 0, rim - 1)], branch, row, half, sem))

                @pl.when(start >= rows)
                def _():
                    act(copy(below.at[branch, jnp.clip(start - rows, 0, rim - 1)], branch, row, half, sem))

                @pl.when((start >= 0) & (start < rows))
                def _():
                    act(copy(own.at[jnp.clip(start, 0, rows - 1)], branch, row, half, sem))

    @pl.loop(0, rows)
    def _(row):
        each(row, lambda copy: copy.start())

    shift = info[2]
    first = pl.multiple_of(jnp.where(shift > 0, 0, 2 * cols - WIN), WIN)
    own_edge = (shift > 0) == (info[1] == 0)

    @pl.loop(0, rows)
    def _(row):
        each(row, lambda copy: copy.wait())
        slot = lax.broadcasted_iota(jnp.int32, (WIN, out_ref.shape[3]), 0)
        taken = jnp.where(shift > 0, slot - shift, WIN + shift - 1 - slot) < 0
        for branch in range(2):
            edge = jnp.where(own_edge, mine_ref[branch, row], other_ref[branch, row])
            edge = edge.astype(jnp.float32)
            place = pl.ds(first, WIN)
            held = out_ref[branch, row, place].astype(jnp.float32)
            both = jnp.concatenate([edge, edge], axis=0)
            out_ref[branch, row, place] = jnp.where(taken, both, held).astype(out_ref.dtype)


def shifted_tokens(lat_cond, lat_uncond, shifts, after, taps):
    core = lax.axis_index("core")
    rows, cols, width = lat_cond.shape
    pair = [lat_cond, lat_uncond]
    shift_rows = shifts[0, 0]
    late = list(lax.optimization_barrier((lat_cond, lat_uncond, after))[:2])
    twin = [cyc(lat_cond, "core", 1), cyc(lat_uncond, "core", 1)]
    above = cyc(jnp.stack([x[rows - RIM :] for x in late]), "ha", 1)
    below = cyc(jnp.stack([x[:RIM] for x in late]), "ha", -1)
    halves = pair + [above, below]
    halves += twin + [cyc(above, "core", 1), cyc(below, "core", 1)]
    low = jnp.stack([x[:, :RIM] for x in late]), above[:, :, :RIM], below[:, :, :RIM]
    high = [jnp.stack([x[:, cols - RIM :] for x in late])]
    high += [above[:, :, cols - RIM :], below[:, :, cols - RIM :]]
    own, up, dn = (jnp.where(core == 0, a, b) for a, b in zip(low, high))
    tall = jnp.concatenate([up, own, dn], axis=1)
    start = (RIM + shift_rows).astype(jnp.uint32)
    edge = lax.dynamic_slice_in_dim(tall, start, rows, axis=1)
    mine = cyc(edge, "wy", 1)
    other = cyc(mine, "core", 1)
    return pl.pallas_call(
        rows_kernel,
        in_specs=[pl.BlockSpec(memory_space=pltpu.SMEM)]
        + [pl.BlockSpec(memory_space=pltpu.VMEM)] * 2
        + [pl.BlockSpec(memory_space=pl.ANY)] * (len(halves) + len(taps)),
        out_specs=pl.BlockSpec(memory_space=pltpu.VMEM),
        out_shape=jax.ShapeDtypeStruct((2, rows, 2 * cols, width), lat_cond.dtype),
        scratch_shapes=[pltpu.SemaphoreType.DMA((rows, 4))],
        cost_estimate=pl.CostEstimate(
            flops=0, transcendentals=0, bytes_accessed=16 * rows * cols * width
        ),
    )(shifts, mine, other, *halves, *taps)


def refined_part(attended, taps, shift_rows, shift_cols):
    _, rows, cols, _ = attended.shape
    rim = RIM + 1
    above = cyc(attended[:, rows - rim :], "ha", 1)
    below = cyc(attended[:, :rim], "ha", -1)
    tall = jnp.concatenate([above, attended, below], axis=1)
    start = (RIM - shift_rows).astype(jnp.uint32)
    tall = lax.dynamic_slice_in_dim(tall, start, rows + 2, axis=1)
    ha, wy = lax.axis_index("ha"), lax.axis_index("wy")
    row = lax.broadcasted_iota(jnp.int32, (1, rows + 2, 1, 1), 1)
    inside = ((row > 0) | (ha > 0)) & ((row < rows + 1) | (ha < lax.axis_size("ha") - 1))
    tall = jnp.where(inside, tall, jnp.zeros_like(tall))
    first, last = tall[:, :, :1], tall[:, :, cols - 1 :]
    sent = jnp.where(
        shift_cols >= 0,
        jnp.concatenate([tall[:, :, :RIM], last], axis=2),
        jnp.concatenate([tall[:, :, cols - RIM :], first], axis=2),
    )
    got = cyc(sent, "wy", 1)
    blank = jnp.zeros(tall.shape[:2] + (cols - 2 * RIM,) + tall.shape[3:], tall.dtype)
    spread = jnp.concatenate([got[:, :, :RIM], blank, got[:, :, :RIM]], axis=2)
    slot = lax.broadcasted_iota(jnp.int32, (1, 1, cols, 1), 2)
    centre = jnp.where((slot < shift_cols) | (slot >= cols + shift_cols), spread, tall)
    left = jnp.where(shift_cols < 0, last, got[:, :, RIM:])
    right = jnp.where(
        shift_cols > 0, first, jnp.where(shift_cols < 0, got[:, :, RIM:], got[:, :, :1])
    )
    left = jnp.where(wy > 0, left, jnp.zeros_like(left))
    right = jnp.where(wy < lax.axis_size("wy") - 1, right, jnp.zeros_like(right))
    wide = jnp.concatenate([left, centre, right], axis=2)
    summed = wide[:, 1 : rows + 1, 1 : cols + 1].astype(jnp.float32)
    for i in range(3):
        for j in range(3):
            part = wide[:, i : i + rows, j : j + cols].astype(jnp.float32)
            summed = summed + taps[i, j] * part
    return summed.astype(jnp.bfloat16)


def on_device(latent_cond, latent_uncond, qkv_weight, cond_pairs, guide_mask, shifts, kernel):
    _, frames, rows, cols, width_d = latent_cond.shape
    assert frames == 1 and rows == 2 * WIN
    heads = qkv_weight.shape[1] // (3 * HD)
    core = lax.axis_index("core")
    shift_rows, shift_cols = shifts[0, 0], shifts[0, 1]
    info = shifts, guide_mask, cyc(guide_mask, "core", 1)
    mine, other = core_halves(qkv_weight, heads, CHUNKS)
    block = ordered(core, mine, cyc(other, "core", 1), 0)
    chips = (lax.axis_size("clip"), lax.axis_size("wy"))
    firsts = [sum(CHUNKS[:i]) for i in range(len(CHUNKS))]
    tags = "abcde"[: len(CHUNKS)]
    held = (block, latent_cond, latent_uncond, cond_pairs)
    block, latent_cond, latent_uncond, cond_pairs = lax.optimization_barrier(held)
    weights = []
    for tag, first, count in zip(tags, firsts, CHUNKS):
        columns = block[:, 3 * first * HD : 3 * (first + count) * HD]
        weights.append(weight_pieces(columns, tag, chips))
    taps = []
    for first, count in zip(firsts, CHUNKS):
        at = ((core * (heads // 2) + first) * HD).astype(jnp.uint32)
        taps.append(lax.dynamic_slice_in_dim(kernel, at, count * HD, axis=2))
    tokens = shifted_tokens(
        latent_cond[0, 0], latent_uncond[0, 0], shifts, weights[0][3], taps
    )
    tokens = tokens.reshape(-1, width_d)
    far = gathered_pairs(cond_pairs[0], heads)
    parts, others = [], []
    for tag, first, count, weight, part_taps in zip(tags, firsts, CHUNKS, weights, taps):
        projected = project(tokens, *weight[:3])
        attended = attend(info, projected, far, first, count, 2 * cols)
        attended = attended.reshape(2, rows, 2 * cols, count * HD)
        part = refined_part(attended, part_taps, shift_rows, shift_cols)
        low, high = part[:, :, :cols], part[:, :, cols:]
        parts.append(jnp.where(core == 0, low, high))
        others.append(cyc(jnp.where(core == 0, high, low), "core", 1))
    out = ordered(core, jnp.concatenate(parts, -1), jnp.concatenate(others, -1), -1)
    return out[None, :, None]


def solution(mesh):
    clips, has, was = (mesh.shape[a] for a in ("clip", "ha", "wa"))
    split = Mesh(mesh.devices.reshape(clips, has, was // 2, 2), ("clip", "ha", "wy", "core"))
    wa = ("wy", "core")
    placed = (
        P("clip", None, "ha", wa, None),
        P("clip", None, "ha", wa, None),
        P(("clip", "ha") + wa, None),
        P("clip", None, ("ha",) + wa, None),
        P("clip", ("ha",) + wa),
        P("clip", None),
        P(),
    )

    return jax.shard_map(
        on_device,
        mesh=split,
        in_specs=placed,
        out_specs=P("clip", None, None, "ha", wa, None),
        check_vma=False,
    )
```
